256 devices in a mesh: blk: 32 (over z, y_lo, core), head: 8 (over x, y_hi).
Axes of the slice: x: 4, y: 4 (y_hi: 2, y_lo: 2; y = y_hi * 2 + y_lo), z: 8, core: 2. Of those that a mesh axis runs over, the one named last changes fastest.
Arguments:
- query: bfloat16 [32768, 4096], P(('blk', 'head')), may hold values from -6 to 6
- key: bfloat16 [32768, 1024], P(('blk', 'head')), may hold values from -6 to 6
- value: bfloat16 [32768, 1024], P(('blk', 'head')), may hold values from -6 to 6
- grad_out: bfloat16 [32768, 4096], P(('blk', 'head')), may hold values from -6 to 6
- doc_lengths: int32 [64], replicated, may hold values from 1 to 1024, 32768 in all
Outputs:
- attended: bfloat16 [32768, 4096], P(('blk', 'head'))
- grad_query: bfloat16 [32768, 4096], P(('blk', 'head'))
- grad_key: bfloat16 [32768, 1024], P(('blk', 'head'))
- grad_value: bfloat16 [32768, 1024], P(('blk', 'head'))
The draws below stay inside these ranges and needn't reach their ends.
Inputs may be any that keep to these rules, and one draw needn't show every extreme that they name: `doc_lengths`: every document has at most 1024 tokens, one has exactly 1024, and the lengths sum to 32768.
All inputs are finite; a program needn't handle non-finite values.
Results may differ from the reference program's by a relative error of at most 0.0088.
Values may be sent and summed in bfloat16 or wider, within the bound.
No kernel may reach another device: no remote copies, remote signals or barrier semaphores. Data moves between devices by JAX's collectives and lax.ppermute only.
A program may use at most 128 MiB of HBM per device.

```python
import math
import jax
import jax.numpy as jnp
import numpy as np
from jax import lax

HEADS = 32
KV_HEADS = 8
HEAD_DIM = 128
BLOCK = 1024
SEQ = 32768
DOC_MOST = 1024
DOCS = 64


def draw_query(key, part):
    entry_key = jax.random.fold_in(key, 11)
    result = jnp.clip(jax.random.normal(entry_key, (SEQ, HEADS * HEAD_DIM), jnp.float32), -4.0, 4.0)
    return result.astype(jnp.bfloat16)


def draw_key(key, part):
    entry_key = jax.random.fold_in(key, 12)
    result = jnp.clip(jax.random.normal(entry_key, (SEQ, KV_HEADS * HEAD_DIM), jnp.float32), -4.0, 4.0)
    return result.astype(jnp.bfloat16)


def levels(own_key, dims, shards, low, high):
    factor_of, own = 1.0, jax.random.fold_in(own_key, 6)
    for axis_at, parts in shards:
        heights = jnp.exp(jax.random.uniform(jax.random.fold_in(own, axis_at), (parts,), jnp.float32, low / len(shards), high / len(shards)))
        factor_of = factor_of * jnp.repeat(heights, dims[axis_at] // parts).reshape([-1 if axis == axis_at else 1 for axis in range(len(dims))])
    return factor_of


def split_up(amount, total, limit, lean):
    loads = [(1 << 20) // math.isqrt(rank ** lean) + 1 for rank in range(2, amount + 1)]
    surplus, holding = total - limit - (amount - 1), [1] * (amount - 1)
    while surplus > 0:
        movable = [i for i in range(amount - 1) if holding[i] < limit]
        mass, budget = sum([loads[i] for i in movable]), surplus
        for i in movable:
            extra = min(limit - holding[i], max(1, budget * loads[i] // mass), surplus)
            holding[i] = holding[i] + extra
            surplus = surplus - extra
    return np.array([limit] + holding)


def uneven_parts(stream_key, amount, total, reach, lean):
    if amount == 2:
        one = jax.random.randint(stream_key, (), max(1, total - reach), min(reach, total - 1) + 1)
        return jnp.stack([one, total - one])
    tallies = jnp.asarray(split_up(amount, total, reach, lean), jnp.int32)
    couples = (amount - 1) // 2
    source_of, sink = tallies[1:1 + 2 * couples:2], tallies[2:2 + 2 * couples:2]
    margin = jnp.minimum(source_of - 1, reach - sink)
    moved = jax.random.randint(jax.random.fold_in(stream_key, 1), (couples,), 0, 1 << 20) % (margin + 1)
    tallies = tallies.at[1:1 + 2 * couples:2].set(source_of - moved).at[2:2 + 2 * couples:2].set(sink + moved)
    return tallies[jax.random.permutation(jax.random.fold_in(stream_key, 2), amount)]


def gaussian(key, extent, scale, most, split=(), kind=jnp.bfloat16):
    loudness = levels(key, extent, split, -0.22, 0.18) if split else 1.0
    values = jax.random.normal(key, extent, jnp.float32) * scale * loudness
    return jnp.minimum(jnp.maximum(values, -most), most).astype(kind)


def setup_inputs(seed: int = 0) -> dict:
    keys = jax.random.split(jax.random.key(seed), 6)
    query = draw_query(jax.random.fold_in(keys[5], 71), 0)
    key = draw_key(jax.random.fold_in(keys[5], 71), 0)
    value = gaussian(keys[2], (SEQ, KV_HEADS * HEAD_DIM), 1.0, 6.0, ((0, 256),))
    grad_out = gaussian(keys[3], (SEQ, HEADS * HEAD_DIM), 1.0, 6.0, ((0, 256),))
    doc_lengths = uneven_parts(keys[4], DOCS, SEQ, DOC_MOST, 2).astype(jnp.int32)
    return {"query": query, "key": key, "value": value, "grad_out": grad_out, "doc_lengths": doc_lengths}


def segment_ids(positions, doc_starts):
    return jnp.sum((doc_starts[None, :] <= positions[:, None]).astype(jnp.int32), axis=1) - 1


def reference(query, key, value, grad_out, doc_lengths):
    scaling = HEAD_DIM ** -0.5
    groups = HEADS // KV_HEADS
    row_step = min(512, BLOCK)
    span_rows = DOC_MOST + row_step
    doc_ends = jnp.cumsum(doc_lengths).astype(jnp.int32)
    doc_starts = (doc_ends - doc_lengths).astype(jnp.int32)
    padding = jnp.zeros((DOC_MOST, KV_HEADS * HEAD_DIM), key.dtype)
    keys_padded = jnp.concatenate([padding, key], axis=0)
    values_padded = jnp.concatenate([padding, value], axis=0)
    offsets = jnp.arange(row_step, dtype=jnp.int32)
    reaches = jnp.arange(span_rows, dtype=jnp.int32)

    def visit(carry, tile_number):
        grad_keys, grad_values = carry
        first_row = (tile_number * row_step).astype(jnp.int32)
        query_rows = lax.dynamic_slice_in_dim(query, first_row, row_step, 0).astype(jnp.float32).reshape(row_step, KV_HEADS, groups, HEAD_DIM)
        grad_rows = lax.dynamic_slice_in_dim(grad_out, first_row, row_step, 0).astype(jnp.float32).reshape(row_step, KV_HEADS, groups, HEAD_DIM)
        key_rows = lax.dynamic_slice_in_dim(keys_padded, first_row, span_rows, 0).astype(jnp.float32).reshape(span_rows, KV_HEADS, HEAD_DIM)
        value_rows = lax.dynamic_slice_in_dim(values_padded, first_row, span_rows, 0).astype(jnp.float32).reshape(span_rows, KV_HEADS, HEAD_DIM)
        query_pos = first_row + offsets
        key_pos = first_row - DOC_MOST + reaches
        allowed = (key_pos[None, :] <= query_pos[:, None]) & (segment_ids(query_pos, doc_starts)[:, None] == segment_ids(key_pos, doc_starts)[None, :])
        scores = jnp.einsum('qkgd,skd->kgqs', query_rows, key_rows) * scaling
        scores = jnp.where(allowed[None, None], scores, -jnp.inf)
        peak_score = jnp.max(scores, axis=-1, keepdims=True)
        log_total = peak_score + jnp.log(jnp.sum(jnp.exp(scores - peak_score), axis=-1, keepdims=True))
        weights = jnp.exp(scores - log_total)
        weights_bf = lax.optimization_barrier(weights.astype(jnp.bfloat16)).astype(jnp.float32)
        attended_rows = jnp.einsum('kgqs,skd->qkgd', weights_bf, value_rows).astype(jnp.bfloat16)
        output_rows = lax.optimization_barrier(attended_rows).astype(jnp.float32)
        row_delta = jnp.einsum('qkgd,qkgd->kgq', grad_rows, output_rows)
        grad_weights = jnp.einsum('qkgd,skd->kgqs', grad_rows, value_rows)
        grad_scores = weights * (grad_weights - row_delta[..., None])
        grad_scores = lax.optimization_barrier(grad_scores.astype(jnp.bfloat16)).astype(jnp.float32)
        grad_query_rows = (jnp.einsum('kgqs,skd->qkgd', grad_scores, key_rows) * scaling).astype(jnp.bfloat16)
        key_part = (jnp.einsum('kgqs,qkgd->skd', grad_scores, query_rows) * scaling).reshape(span_rows, KV_HEADS * HEAD_DIM)
        value_part = jnp.einsum('kgqs,qkgd->skd', weights_bf, grad_rows).reshape(span_rows, KV_HEADS * HEAD_DIM)
        current_keys = lax.dynamic_slice_in_dim(grad_keys, first_row, span_rows, 0)
        current_values = lax.dynamic_slice_in_dim(grad_values, first_row, span_rows, 0)
        grad_keys = lax.dynamic_update_slice_in_dim(grad_keys, current_keys + key_part, first_row, 0)
        grad_values = lax.dynamic_update_slice_in_dim(grad_values, current_values + value_part, first_row, 0)
        outputs = (attended_rows.reshape(row_step, HEADS * HEAD_DIM), grad_query_rows.reshape(row_step, HEADS * HEAD_DIM))
        return (grad_keys, grad_values), outputs

    start_keys = jnp.zeros((SEQ + DOC_MOST, KV_HEADS * HEAD_DIM), jnp.float32)
    start_values = jnp.zeros((SEQ + DOC_MOST, KV_HEADS * HEAD_DIM), jnp.float32)
    tile_numbers = jnp.arange(SEQ // row_step, dtype=jnp.int32)
    sums, stacked = lax.scan(visit, (start_keys, start_values), tile_numbers)
    attended = stacked[0].reshape(SEQ, HEADS * HEAD_DIM)
    grad_query = stacked[1].reshape(SEQ, HEADS * HEAD_DIM)
    grad_key = sums[0][DOC_MOST:].astype(jnp.bfloat16)
    grad_value = sums[1][DOC_MOST:].astype(jnp.bfloat16)
    return (attended, grad_query, grad_key, grad_value)
```

```python
import functools
import math

import jax
import jax.numpy as jnp
from jax import lax
from jax.experimental import pallas as pl
from jax.experimental.pallas import tpu as pltpu
from jax.sharding import PartitionSpec as P

HEAD_DIM = 128
SCALE = HEAD_DIM**-0.5
SCALE_LOG2 = SCALE * math.log2(math.e)
FLOOR = -1e30
TILE_Q = 256
TILE_K = 256
LAST_DIMS = (((1,), (1,)), ((), ()))


def passed_along(value, axis, steps):
    count = lax.axis_size(axis)
    initial, last = (max(0, -steps), min(count, count - steps))
    return lax.ppermute(value, axis, [(source, source + steps) for source in range(initial, last)])


def attention_kernel(heads, block, first, last, lo_ref, start_ref, rows_ref, earlier_ref, own_ref, *refs):
    if first:
        carried_ref = None
    else:
        carried_ref, refs = refs[0], refs[1:]
    out_ref, refs = refs[0], refs[1:]
    if last:
        earlier_out, own_out, refs = refs[0], refs[1], refs[2:]
    else:
        sums_out, refs = refs[0], refs[1:]
    window, scores, sums, peaks, totals, attended, grad_query = refs
    tile, tiles = pl.program_id(0), pl.num_programs(0)
    stacked = heads * TILE_Q

    @pl.when(tile == 0)
    def _():
        window[:block] = earlier_ref[...]
        window[block:] = own_ref[...]
        sums[...] = jnp.zeros_like(sums) if first else carried_ref[...]

    lo = lo_ref[tile]
    hi = (block + (tile + 1) * TILE_Q - 1) // TILE_K + 1

    def stack(base):
        return jnp.concatenate(
            [rows_ref[:, base + h * HEAD_DIM : base + (h + 1) * HEAD_DIM] for h in range(heads)], axis=0
        )

    query = stack(0)
    grad = stack(heads * HEAD_DIM)
    row = block + tile * TILE_Q + lax.broadcasted_iota(jnp.int32, (TILE_Q, TILE_K), 0)
    start = start_ref[...]
    peaks[...] = jnp.full_like(peaks, FLOOR)
    totals[...] = jnp.zeros_like(totals)
    attended[...] = jnp.zeros_like(attended)
    grad_query[...] = jnp.zeros_like(grad_query)

    @pl.loop(lo, hi)
    def _(step):
        base = pl.multiple_of(step * TILE_K, TILE_K)
        product = lax.dot_general(
            query, window[pl.ds(base, TILE_K), :HEAD_DIM], LAST_DIMS, preferred_element_type=jnp.float32
        )
        column = base + lax.broadcasted_iota(jnp.int32, (TILE_Q, TILE_K), 1)
        kept = (column <= row) & (column >= start)
        product = jnp.where(kept[None], product.reshape(heads, TILE_Q, TILE_K) * SCALE_LOG2, FLOOR)
        product = product.reshape(stacked, TILE_K)
        scores[step - lo] = product
        peak = peaks[...]
        for j in range(TILE_K // 128):
            peak = jnp.maximum(peak, product[:, j * 128 : (j + 1) * 128])
        peaks[...] = peak

    peak = jnp.max(peaks[...], axis=1, keepdims=True)

    @pl.loop(lo, hi)
    def _(step):
        base = pl.multiple_of(step * TILE_K, TILE_K)
        weights = jnp.exp2(scores[step - lo] - peak)
        scores[step - lo] = weights
        total = totals[...]
        for j in range(TILE_K // 128):
            total = total + weights[:, j * 128 : (j + 1) * 128]
        totals[...] = total
        attended[...] += jnp.dot(
            weights.astype(jnp.bfloat16), window[pl.ds(base, TILE_K), HEAD_DIM:], preferred_element_type=jnp.float32
        )

    inverse = 1.0 / jnp.sum(totals[...], axis=1, keepdims=True)
    out = (attended[...] * inverse).astype(jnp.bfloat16)
    grad_wide = grad.astype(jnp.float32)
    delta = jnp.sum(grad_wide * out.astype(jnp.float32), axis=1, keepdims=True)
    grad_across = (grad_wide * inverse).astype(jnp.bfloat16).T
    query_across = (query.astype(jnp.float32) * (inverse * SCALE)).astype(jnp.bfloat16).T

    @pl.loop(lo, hi)
    def _(step):
        base = pl.multiple_of(step * TILE_K, TILE_K)
        span = pl.ds(base, TILE_K)
        keys = window[span, :HEAD_DIM]
        weights = scores[step - lo]
        grad_weights = lax.dot_general(grad, window[span, HEAD_DIM:], LAST_DIMS, preferred_element_type=jnp.float32)
        grad_scores = (weights * (grad_weights - delta)).astype(jnp.bfloat16)
        grad_query[...] += jnp.dot(grad_scores, keys, preferred_element_type=jnp.float32)
        sums[:HEAD_DIM, span] += jnp.dot(query_across, grad_scores, preferred_element_type=jnp.float32)
        sums[HEAD_DIM:, span] += jnp.dot(
            grad_across, weights.astype(jnp.bfloat16), preferred_element_type=jnp.float32
        )

    grad_rows = (grad_query[...] * (inverse * SCALE)).astype(jnp.bfloat16)
    for h in range(heads):
        out_ref[:, h * HEAD_DIM : (h + 1) * HEAD_DIM] = out[h * TILE_Q : (h + 1) * TILE_Q]
        out_ref[:, (heads + h) * HEAD_DIM : (heads + h + 1) * HEAD_DIM] = grad_rows[h * TILE_Q : (h + 1) * TILE_Q]

    @pl.when(tile == tiles - 1)
    def _():
        if last:
            earlier_out[...] = sums[:, :block].astype(jnp.bfloat16).T
            own_out[...] = sums[:, block:].T
        else:
            sums_out[...] = sums[...]


def attention(rows, earlier, own, carried, start, lo, last):
    block, width = rows.shape
    heads = width // (2 * HEAD_DIM)
    pair = own.shape[1]
    stacked = heads * TILE_Q
    most = block // TILE_K + 1
    first = carried is None
    whole = lambda t, _: (0, 0)
    by_tile = lambda t, _: (t, 0)
    in_specs = [
        pl.BlockSpec((TILE_Q, 1), by_tile),
        pl.BlockSpec((TILE_Q, width), by_tile),
        pl.BlockSpec((block, pair), whole),
        pl.BlockSpec((block, pair), whole),
    ]
    operands = [start, rows, earlier, own]
    if not first:
        in_specs.append(pl.BlockSpec((pair, 2 * block), whole))
        operands.append(carried)
    out_specs = [pl.BlockSpec((TILE_Q, width), by_tile)]
    out_shape = [jax.ShapeDtypeStruct((block, width), jnp.bfloat16)]
    if last:
        out_specs += [pl.BlockSpec((block, pair), whole)] * 2
        out_shape += [
            jax.ShapeDtypeStruct((block, pair), jnp.bfloat16),
            jax.ShapeDtypeStruct((block, pair), jnp.float32),
        ]
    else:
        out_specs.append(pl.BlockSpec((pair, 2 * block), whole))
        out_shape.append(jax.ShapeDtypeStruct((pair, 2 * block), jnp.float32))
    pairs = heads * block * block
    return pl.pallas_call(
        functools.partial(attention_kernel, heads, block, first, last),
        grid_spec=pltpu.PrefetchScalarGridSpec(
            num_scalar_prefetch=1,
            grid=(block // TILE_Q,),
            in_specs=in_specs,
            out_specs=out_specs,
            scratch_shapes=[
                pltpu.VMEM((2 * block, pair), jnp.bfloat16),
                pltpu.VMEM((most, stacked, TILE_K), jnp.float32),
                pltpu.VMEM((pair, 2 * block), jnp.float32),
                pltpu.VMEM((stacked, 128), jnp.float32),
                pltpu.VMEM((stacked, 128), jnp.float32),
                pltpu.VMEM((stacked, HEAD_DIM), jnp.float32),
                pltpu.VMEM((stacked, HEAD_DIM), jnp.float32),
            ],
        ),
        out_shape=out_shape,
        compiler_params=pltpu.CompilerParams(vmem_limit_bytes=40 << 20),
        cost_estimate=pl.CostEstimate(
            flops=12 * pairs * HEAD_DIM, bytes_accessed=4 * block * width, transcendentals=pairs
        ),
        name="attention_" + ("first" if first else "last"),
    )(lo, *operands)


def exchange(value):
    return lax.all_to_all(value, "head", split_axis=0, concat_axis=0, tiled=True)


def per_device(query, key, value, grad_out, doc_lengths):
    rows = query.shape[0]
    count = lax.axis_size("head")
    block = rows * count
    pair = 2 * HEAD_DIM
    groups = query.shape[1] // key.shape[1]
    half = groups // 2
    by_head = lambda x: x.reshape(rows, count, -1)

    doc_ends = jnp.cumsum(doc_lengths)
    doc_starts = doc_ends - doc_lengths
    origin = lax.axis_index("blk") * block - block
    positions = origin + block + jnp.arange(block, dtype=jnp.int32)
    starts = jnp.max(jnp.where(doc_starts[None, :] <= positions[:, None], doc_starts[None, :], 0), axis=1)
    starts = starts - origin
    lo = jnp.maximum(starts[::TILE_Q] // TILE_K, 0).astype(jnp.int32)
    starts = starts.astype(jnp.int32)[:, None]

    key_value = jnp.concatenate([by_head(key), by_head(value)], axis=2).transpose(1, 0, 2)
    own = exchange(key_value).reshape(block, pair)
    earlier = passed_along(own, "blk", 1)

    def entering(g):
        span = slice(g * half * HEAD_DIM, (g + 1) * half * HEAD_DIM)
        packed = jnp.concatenate([by_head(query)[:, :, span], by_head(grad_out)[:, :, span]], axis=2)
        return exchange(packed.transpose(1, 0, 2)).reshape(block, groups * HEAD_DIM)

    rows_first = entering(0)
    rows_last = entering(1)
    out_first, carried = attention(rows_first, earlier, own, None, starts, lo, False)
    back_first = exchange(out_first.reshape(count, rows, -1))
    out_last, earlier_sums, own_sums = attention(rows_last, earlier, own, carried, starts, lo, True)
    back_last = exchange(out_last.reshape(count, rows, -1))
    returned = passed_along(earlier_sums, "blk", -1)
    pair_sums = (own_sums + returned.astype(jnp.float32)).astype(jnp.bfloat16)
    back_pair = exchange(pair_sums.reshape(count, rows, pair))

    middle = half * HEAD_DIM
    attended = jnp.concatenate([back_first[:, :, :middle], back_last[:, :, :middle]], axis=2)
    grad_query = jnp.concatenate([back_first[:, :, middle:], back_last[:, :, middle:]], axis=2)
    flat = lambda x: x.transpose(1, 0, 2).reshape(rows, -1)
    return (
        flat(attended),
        flat(grad_query),
        flat(back_pair[:, :, :HEAD_DIM]),
        flat(back_pair[:, :, HEAD_DIM:]),
    )


def solution(mesh):
    spec = P(("blk", "head"), None)
    return jax.shard_map(
        per_device,
        mesh=mesh,
        in_specs=(spec, spec, spec, spec, P()),
        out_specs=(spec, spec, spec, spec),
        check_vma=False,
    )
```

```python
import functools
import math

import jax
import jax.numpy as jnp
from jax import lax
from jax.experimental import pallas as pl
from jax.experimental.pallas import tpu as pltpu
from jax.sharding import PartitionSpec as P

HEAD_DIM = 128
SCALE = HEAD_DIM**-0.5
SCALE_LOG2 = SCALE * math.log2(math.e)
FLOOR = -1e30
TILE_Q = 128
TILE_K = 256
LAST_DIMS = (((1,), (1,)), ((), ()))


def passed_along(value, axis, steps):
    count = lax.axis_size(axis)
    initial, last = (max(0, -steps), min(count, count - steps))
    return lax.ppermute(value, axis, [(source, source + steps) for source in range(initial, last)])


def attention_kernel(
    heads, block, most, pad, counts_ref, start_ref, rows_ref, earlier_ref, own_ref, out_ref, earlier_out, own_out, window, sums
):
    tile, tiles = pl.program_id(0), pl.num_programs(0)
    stacked = heads * TILE_Q

    @pl.when(tile == 0)
    def _():
        if pad:
            window[:pad] = jnp.zeros((pad, window.shape[1]), window.dtype)
        window[pad : pad + block] = earlier_ref[...]
        window[pad + block :] = own_ref[...]
        sums[...] = jnp.zeros_like(sums)

    def visit(count):
        width = count * TILE_K
        first = block + (tile + 1) * TILE_Q - width
        span = pl.ds(pl.multiple_of(first + pad, 128), width)

        def stack(base):
            return jnp.concatenate(
                [rows_ref[:, base + h * HEAD_DIM : base + (h + 1) * HEAD_DIM] for h in range(heads)], axis=0
            )

        query = stack(0)
        grad = stack(heads * HEAD_DIM)
        keys = window[span, :HEAD_DIM]
        values = window[span, HEAD_DIM:]
        scores = lax.dot_general(query, keys, LAST_DIMS, preferred_element_type=jnp.float32)
        row = block + tile * TILE_Q + lax.broadcasted_iota(jnp.int32, (TILE_Q, width), 0)
        column = first + lax.broadcasted_iota(jnp.int32, (TILE_Q, width), 1)
        kept = (column <= row) & (column >= start_ref[...])
        scores = jnp.where(kept[None], scores.reshape(heads, TILE_Q, width) * SCALE_LOG2, FLOOR)
        scores = scores.reshape(stacked, width)
        weights = jnp.exp2(scores - jnp.max(scores, axis=1, keepdims=True))
        inverse = 1.0 / jnp.sum(weights, axis=1, keepdims=True)
        weights_bf = weights.astype(jnp.bfloat16)
        out = (jnp.dot(weights_bf, values, preferred_element_type=jnp.float32) * inverse).astype(jnp.bfloat16)
        grad_wide = grad.astype(jnp.float32)
        delta = jnp.sum(grad_wide * out.astype(jnp.float32), axis=1, keepdims=True)
        grad_weights = lax.dot_general(grad, values, LAST_DIMS, preferred_element_type=jnp.float32)
        grad_scores = (weights * (grad_weights - delta)).astype(jnp.bfloat16)
        grad_query = jnp.dot(grad_scores, keys, preferred_element_type=jnp.float32) * (inverse * SCALE)
        grad_query = grad_query.astype(jnp.bfloat16)
        grad_scaled = (grad_wide * inverse).astype(jnp.bfloat16)
        query_scaled = (query.astype(jnp.float32) * (inverse * SCALE)).astype(jnp.bfloat16)
        sums[:HEAD_DIM, span] += jnp.dot(query_scaled.T, grad_scores, preferred_element_type=jnp.float32)
        sums[HEAD_DIM:, span] += jnp.dot(grad_scaled.T, weights_bf, preferred_element_type=jnp.float32)
        for h in range(heads):
            picked = slice(h * TILE_Q, (h + 1) * TILE_Q)
            out_ref[:, h * HEAD_DIM : (h + 1) * HEAD_DIM] = out[picked]
            out_ref[:, (heads + h) * HEAD_DIM : (heads + h + 1) * HEAD_DIM] = grad_query[picked]

    needed = counts_ref[tile]
    for count in range(1, most + 1):
        pl.when(needed == count)(functools.partial(visit, count))

    @pl.when(tile == tiles - 1)
    def _():
        earlier_out[...] = sums[:, pad : pad + block].astype(jnp.bfloat16).T
        own_out[...] = sums[:, pad + block :].T


def attention(entered, earlier, starts):
    block, pair = earlier.shape
    whole_width = entered.shape[1]
    width = whole_width - pair
    heads = width // (2 * HEAD_DIM)
    most = -(-(TILE_Q + block - 1) // TILE_K)
    pad = max(0, most * TILE_K - block - TILE_Q)
    ends = block + TILE_Q * jnp.arange(1, block // TILE_Q + 1, dtype=jnp.int32)
    counts = jnp.clip((ends - starts[::TILE_Q] + TILE_K - 1) // TILE_K, 1, most).astype(jnp.int32)
    whole = lambda t, _: (0, 0)
    by_tile = lambda t, _: (t, 0)
    pairs = heads * block * block
    return pl.pallas_call(
        functools.partial(attention_kernel, heads, block, most, pad),
        grid_spec=pltpu.PrefetchScalarGridSpec(
            num_scalar_prefetch=1,
            grid=(block // TILE_Q,),
            in_specs=[
                pl.BlockSpec((TILE_Q, 1), by_tile),
                pl.BlockSpec((TILE_Q, width), by_tile),
                pl.BlockSpec((block, pair), whole),
                pl.BlockSpec((block, pair), lambda t, _: (0, width // pair)),
            ],
            out_specs=[
                pl.BlockSpec((TILE_Q, width), by_tile),
                pl.BlockSpec((block, pair), whole),
                pl.BlockSpec((block, pair), whole),
            ],
            scratch_shapes=[
                pltpu.VMEM((pad + 2 * block, pair), jnp.bfloat16),
                pltpu.VMEM((pair, pad + 2 * block), jnp.float32),
            ],
        ),
        out_shape=[
            jax.ShapeDtypeStruct((block, whole_width), jnp.bfloat16),
            jax.ShapeDtypeStruct((block, pair), jnp.bfloat16),
            jax.ShapeDtypeStruct((block, pair), jnp.float32),
        ],
        compiler_params=pltpu.CompilerParams(vmem_limit_bytes=32 << 20),
        cost_estimate=pl.CostEstimate(
            flops=12 * pairs * HEAD_DIM, bytes_accessed=4 * block * width, transcendentals=pairs
        ),
        name="attention",
    )(counts, starts[:, None], entered, earlier, entered)


def exchange(value):
    return lax.all_to_all(value, "head", split_axis=0, concat_axis=0, tiled=True)


def per_device(query, key, value, grad_out, doc_lengths):
    rows = query.shape[0]
    count = lax.axis_size("head")
    block = rows * count
    pair = 2 * HEAD_DIM
    middle = query.shape[1] // count
    by_head = lambda x: x.reshape(rows, count, -1)
    flat = lambda x: x.transpose(1, 0, 2).reshape(rows, -1)

    doc_ends = jnp.cumsum(doc_lengths)
    doc_starts = doc_ends - doc_lengths
    origin = lax.axis_index("blk") * block - block
    positions = origin + block + jnp.arange(block, dtype=jnp.int32)
    starts = jnp.max(jnp.where(doc_starts[None, :] <= positions[:, None], doc_starts[None, :], 0), axis=1)
    starts = (starts - origin).astype(jnp.int32)

    packed = jnp.concatenate([by_head(x) for x in (query, grad_out, key, value)], axis=2).transpose(1, 0, 2)
    entered = exchange(packed).reshape(block, -1)
    earlier = passed_along(entered[:, 2 * middle :], "blk", 1)
    out, earlier_sums, own_sums = attention(entered, earlier, starts)
    returned = passed_along(earlier_sums, "blk", -1)
    pair_sums = (own_sums + returned.astype(jnp.float32)).astype(jnp.bfloat16)
    out = lax.dynamic_update_slice(out, pair_sums, (0, 2 * middle))
    back = exchange(out.reshape(count, rows, -1))
    edges = (0, middle, 2 * middle, 2 * middle + HEAD_DIM, 2 * middle + pair)
    return tuple(flat(back[:, :, left:right]) for left, right in zip(edges[:-1], edges[1:]))


def solution(mesh):
    spec = P(("blk", "head"), None)
    return jax.shard_map(
        per_device,
        mesh=mesh,
        in_specs=(spec, spec, spec, spec, P()),
        out_specs=(spec, spec, spec, spec),
        check_vma=False,
    )
```

```python
import functools
import math

import jax
import jax.numpy as jnp
from jax import lax
from jax.experimental import pallas as pl
from jax.experimental.pallas import tpu as pltpu
from jax.sharding import PartitionSpec as P

HEAD_DIM = 128
SCALE = HEAD_DIM**-0.5
SCALE_LOG2 = SCALE * math.log2(math.e)
FLOOR = -1e30
TILE_Q = 128
TILE_K = 128
LAST_DIMS = (((1,), (1,)), ((), ()))


def passed_along(value, axis, steps):
    count = lax.axis_size(axis)
    initial, last = (max(0, -steps), min(count, count - steps))
    return lax.ppermute(value, axis, [(source, source + steps) for source in range(initial, last)])


def attention_kernel(
    heads, block, most, pad, counts_ref, start_ref, entered, earlier_ref, out_ref, earlier_out, own_out, window, sums
):
    stacked = heads * TILE_Q
    wide = 2 * heads * HEAD_DIM
    if pad:
        window[:pad] = jnp.zeros((pad, window.shape[1]), window.dtype)
    window[pad : pad + block] = earlier_ref[...]
    window[pad + block :] = entered[:, wide:]
    sums[...] = jnp.zeros_like(sums)

    def visit(count, tile):
        width = count * TILE_K
        first = block + (tile + 1) * TILE_Q - width
        span = pl.ds(pl.multiple_of(first + pad, 128), width)
        picked = pl.ds(pl.multiple_of(tile * TILE_Q, TILE_Q), TILE_Q)

        def stack(base):
            return jnp.concatenate(
                [entered[picked, base + h * HEAD_DIM : base + (h + 1) * HEAD_DIM] for h in range(heads)], axis=0
            )

        query = stack(0)
        grad = stack(heads * HEAD_DIM)
        keys = window[span, :HEAD_DIM]
        values = window[span, HEAD_DIM:]
        scores = lax.dot_general(query, keys, LAST_DIMS, preferred_element_type=jnp.float32)
        row = block + tile * TILE_Q + lax.broadcasted_iota(jnp.int32, (TILE_Q, width), 0)
        column = first + lax.broadcasted_iota(jnp.int32, (TILE_Q, width), 1)
        kept = (column <= row) & (column >= start_ref[picked, :])
        scores = jnp.where(kept[None], scores.reshape(heads, TILE_Q, width) * SCALE_LOG2, FLOOR)
        scores = scores.reshape(stacked, width)
        weights = jnp.exp2(scores - jnp.max(scores, axis=1, keepdims=True))
        inverse = 1.0 / jnp.sum(weights, axis=1, keepdims=True)
        weights_bf = weights.astype(jnp.bfloat16)
        out = (jnp.dot(weights_bf, values, preferred_element_type=jnp.float32) * inverse).astype(jnp.bfloat16)
        grad_wide = grad.astype(jnp.float32)
        delta = jnp.sum(grad_wide * out.astype(jnp.float32), axis=1, keepdims=True)
        grad_weights = lax.dot_general(grad, values, LAST_DIMS, preferred_element_type=jnp.float32)
        grad_scores = (weights * (grad_weights - delta)).astype(jnp.bfloat16)
        grad_query = jnp.dot(grad_scores, keys, preferred_element_type=jnp.float32) * (inverse * SCALE)
        grad_query = grad_query.astype(jnp.bfloat16)
        grad_scaled = (grad_wide * inverse).astype(jnp.bfloat16)
        query_scaled = (query.astype(jnp.float32) * (inverse * SCALE)).astype(jnp.bfloat16)
        sums[:HEAD_DIM, span] += jnp.dot(query_scaled.T, grad_scores, preferred_element_type=jnp.float32)
        sums[HEAD_DIM:, span] += jnp.dot(grad_scaled.T, weights_bf, preferred_element_type=jnp.float32)
        for h in range(heads):
            part = slice(h * TILE_Q, (h + 1) * TILE_Q)
            out_ref[picked, h * HEAD_DIM : (h + 1) * HEAD_DIM] = out[part]
            out_ref[picked, (heads + h) * HEAD_DIM : (heads + h + 1) * HEAD_DIM] = grad_query[part]

    @pl.loop(0, block // TILE_Q)
    def _(tile):
        needed = counts_ref[tile]
        for count in range(1, most + 1):
            pl.when(needed == count)(functools.partial(visit, count, tile))

    earlier_out[...] = sums[:, pad : pad + block].astype(jnp.bfloat16).T
    own_out[...] = sums[:, pad + block :].T


def attention(entered, earlier, starts):
    block, pair = earlier.shape
    heads = (entered.shape[1] - pair) // (2 * HEAD_DIM)
    most = -(-(TILE_Q + block - 1) // TILE_K)
    pad = max(0, most * TILE_K - block - TILE_Q)
    ends = block + TILE_Q * jnp.arange(1, block // TILE_Q + 1, dtype=jnp.int32)
    counts = jnp.clip((ends - starts[::TILE_Q] + TILE_K - 1) // TILE_K, 1, most).astype(jnp.int32)
    pairs = heads * block * block
    vmem = pl.BlockSpec(memory_space=pltpu.VMEM)
    return pl.pallas_call(
        functools.partial(attention_kernel, heads, block, most, pad),
        in_specs=[pl.BlockSpec(memory_space=pltpu.SMEM), vmem, vmem, vmem],
        out_specs=[vmem, vmem, vmem],
        scratch_shapes=[
            pltpu.VMEM((pad + 2 * block, pair), jnp.bfloat16),
            pltpu.VMEM((pair, pad + 2 * block), jnp.float32),
        ],
        out_shape=[
            jax.ShapeDtypeStruct(entered.shape, jnp.bfloat16),
            jax.ShapeDtypeStruct((block, pair), jnp.bfloat16),
            jax.ShapeDtypeStruct((block, pair), jnp.float32),
        ],
        compiler_params=pltpu.CompilerParams(vmem_limit_bytes=32 << 20),
        cost_estimate=pl.CostEstimate(
            flops=12 * pairs * HEAD_DIM, bytes_accessed=4 * entered.size, transcendentals=pairs
        ),
        name="attention",
    )(counts, starts[:, None], entered, earlier)


def moves(copies, sems):
    started = [pltpu.make_async_copy(source, target, sems.at[i]) for i, (source, target) in enumerate(copies)]
    for copy in started:
        copy.start()
    for copy in started:
        copy.wait()


def portions(count, wholes, joined):
    pairs, at = [], 0
    for whole in wholes:
        width = whole.shape[1] // count
        for h in range(count):
            pairs.append((whole.at[:, pl.ds(h * width, width)], joined.at[h, :, pl.ds(at, width)]))
        at += width
    return pairs


def pack_kernel(count, *refs):
    *wholes, joined, sems = refs
    moves(portions(count, wholes, joined), sems)


def unpack_kernel(count, joined, *refs):
    *wholes, sems = refs
    moves([(target, source) for source, target in portions(count, wholes, joined)], sems)


def pack(count, *wholes):
    rows = wholes[0].shape[0]
    width = sum(x.shape[1] for x in wholes) // count
    return pl.pallas_call(
        functools.partial(pack_kernel, count),
        in_specs=[pl.BlockSpec(memory_space=pl.ANY)] * len(wholes),
        out_specs=pl.BlockSpec(memory_space=pltpu.VMEM),
        out_shape=jax.ShapeDtypeStruct((count, rows, width), wholes[0].dtype),
        scratch_shapes=[pltpu.SemaphoreType.DMA((len(wholes) * count,))],
        name="pack",
    )(*wholes)


def unpack(joined, widths):
    count, rows, _ = joined.shape
    return pl.pallas_call(
        functools.partial(unpack_kernel, count),
        in_specs=[pl.BlockSpec(memory_space=pltpu.VMEM)],
        out_specs=[pl.BlockSpec(memory_space=pl.ANY)] * len(widths),
        out_shape=[jax.ShapeDtypeStruct((rows, count * width), joined.dtype) for width in widths],
        scratch_shapes=[pltpu.SemaphoreType.DMA((len(widths) * count,))],
        name="unpack",
    )(joined)


def exchange(value):
    return lax.all_to_all(value, "head", split_axis=0, concat_axis=0, tiled=True)


def per_device(query, key, value, grad_out, doc_lengths):
    rows = query.shape[0]
    count = lax.axis_size("head")
    block = rows * count
    pair = 2 * HEAD_DIM
    middle = query.shape[1] // count

    doc_ends = jnp.cumsum(doc_lengths)
    doc_starts = doc_ends - doc_lengths
    origin = lax.axis_index("blk") * block - block
    positions = origin + block + jnp.arange(block, dtype=jnp.int32)
    starts = jnp.max(jnp.where(doc_starts[None, :] <= positions[:, None], doc_starts[None, :], 0), axis=1)
    starts = (starts - origin).astype(jnp.int32)

    packed = pack(count, query, grad_out, key, value)
    entered = exchange(packed).reshape(block, -1)
    earlier = passed_along(entered[:, 2 * middle :], "blk", 1)
    out, earlier_sums, own_sums = attention(entered, earlier, starts)
    returned = passed_along(earlier_sums, "blk", -1)
    pair_sums = (own_sums + returned.astype(jnp.float32)).astype(jnp.bfloat16)
    out = lax.dynamic_update_slice(out, pair_sums, (0, 2 * middle))
    back = exchange(out.reshape(count, rows, -1))
    return tuple(unpack(back, (middle, middle, HEAD_DIM, HEAD_DIM)))


def solution(mesh):
    spec = P(("blk", "head"), None)
    return jax.shard_map(
        per_device,
        mesh=mesh,
        in_specs=(spec, spec, spec, spec, P()),
        out_specs=(spec, spec, spec, spec),
        check_vma=False,
    )
```

```python
import functools
import math

import jax
import jax.numpy as jnp
from jax import lax
from jax.experimental import pallas as pl
from jax.experimental.pallas import tpu as pltpu
from jax.sharding import PartitionSpec as P

HEAD_DIM = 128
SCALE = HEAD_DIM**-0.5
SCALE_LOG2 = SCALE * math.log2(math.e)
FLOOR = -1e30
TILE_Q = 128
TILE_K = 128
LAST_DIMS = (((1,), (1,)), ((), ()))


def passed_along(value, axis, steps):
    count = lax.axis_size(axis)
    initial, last = (max(0, -steps), min(count, count - steps))
    return lax.ppermute(value, axis, [(source, source + steps) for source in range(initial, last)])


def attention_kernel(
    heads, block, most, pad, counts_ref, start_ref, entered, earlier_ref, out_ref, earlier_out, own_out, window, sums
):
    stacked = heads * TILE_Q
    wide = 2 * heads * HEAD_DIM
    if pad:
        window[:pad] = jnp.zeros((pad, window.shape[1]), window.dtype)
    window[pad : pad + block] = earlier_ref[...]
    window[pad + block :] = entered[:, wide:]
    sums[...] = jnp.zeros_like(sums)

    def visit(count, tile):
        width = count * TILE_K
        first = block + (tile + 1) * TILE_Q - width
        span = pl.ds(pl.multiple_of(first + pad, 128), width)
        picked = pl.ds(pl.multiple_of(tile * TILE_Q, TILE_Q), TILE_Q)

        def stack(base):
            return jnp.concatenate(
                [entered[picked, base + h * HEAD_DIM : base + (h + 1) * HEAD_DIM] for h in range(heads)], axis=0
            )

        query = stack(0)
        grad = stack(heads * HEAD_DIM)
        keys = window[span, :HEAD_DIM]
        values = window[span, HEAD_DIM:]
        scores = lax.dot_general(query, keys, LAST_DIMS, preferred_element_type=jnp.float32)
        row = block + tile * TILE_Q + lax.broadcasted_iota(jnp.int32, (TILE_Q, width), 0)
        column = first + lax.broadcasted_iota(jnp.int32, (TILE_Q, width), 1)
        kept = (column <= row) & (column >= start_ref[picked, :])
        scores = jnp.where(kept[None], scores.reshape(heads, TILE_Q, width) * SCALE_LOG2, FLOOR)
        scores = scores.reshape(stacked, width)
        weights = jnp.exp2(scores - jnp.max(scores, axis=1, keepdims=True))
        inverse = 1.0 / jnp.sum(weights, axis=1, keepdims=True)
        weights_bf = weights.astype(jnp.bfloat16)
        out = (jnp.dot(weights_bf, values, preferred_element_type=jnp.float32) * inverse).astype(jnp.bfloat16)
        grad_wide = grad.astype(jnp.float32)
        delta = jnp.sum(grad_wide * out.astype(jnp.float32), axis=1, keepdims=True)
        grad_weights = lax.dot_general(grad, values, LAST_DIMS, preferred_element_type=jnp.float32)
        grad_scores = (weights * (grad_weights - delta)).astype(jnp.bfloat16)
        grad_query = jnp.dot(grad_scores, keys, preferred_element_type=jnp.float32) * (inverse * SCALE)
        grad_query = grad_query.astype(jnp.bfloat16)
        grad_scaled = (grad_wide * inverse).astype(jnp.bfloat16)
        query_scaled = (query.astype(jnp.float32) * (inverse * SCALE)).astype(jnp.bfloat16)
        sums[:HEAD_DIM, span] += jnp.dot(query_scaled.T, grad_scores, preferred_element_type=jnp.float32)
        sums[HEAD_DIM:, span] += jnp.dot(grad_scaled.T, weights_bf, preferred_element_type=jnp.float32)
        for h in range(heads):
            part = slice(h * TILE_Q, (h + 1) * TILE_Q)
            out_ref[picked, h * HEAD_DIM : (h + 1) * HEAD_DIM] = out[part]
            out_ref[picked, (heads + h) * HEAD_DIM : (heads + h + 1) * HEAD_DIM] = grad_query[part]

    @pl.loop(0, block // TILE_Q)
    def _(tile):
        needed = counts_ref[tile]
        for count in range(1, most + 1):
            pl.when(needed == count)(functools.partial(visit, count, tile))

    earlier_out[...] = sums[:, pad : pad + block].astype(jnp.bfloat16).T
    own_out[...] = sums[:, pad + block :].T


def attention(entered, earlier, starts):
    block, pair = earlier.shape
    heads = (entered.shape[1] - pair) // (2 * HEAD_DIM)
    most = -(-(TILE_Q + block - 1) // TILE_K)
    pad = max(0, most * TILE_K - block - TILE_Q)
    ends = block + TILE_Q * jnp.arange(1, block // TILE_Q + 1, dtype=jnp.int32)
    counts = jnp.clip((ends - starts[::TILE_Q] + TILE_K - 1) // TILE_K, 1, most).astype(jnp.int32)
    pairs = heads * block * block
    vmem = pl.BlockSpec(memory_space=pltpu.VMEM)
    return pl.pallas_call(
        functools.partial(attention_kernel, heads, block, most, pad),
        in_specs=[pl.BlockSpec(memory_space=pltpu.SMEM), vmem, vmem, vmem],
        out_specs=[vmem, vmem, vmem],
        scratch_shapes=[
            pltpu.VMEM((pad + 2 * block, pair), jnp.bfloat16),
            pltpu.VMEM((pair, pad + 2 * block), jnp.float32),
        ],
        out_shape=[
            jax.ShapeDtypeStruct(entered.shape, jnp.bfloat16),
            jax.ShapeDtypeStruct((block, pair), jnp.bfloat16),
            jax.ShapeDtypeStruct((block, pair), jnp.float32),
        ],
        compiler_params=pltpu.CompilerParams(vmem_limit_bytes=32 << 20),
        cost_estimate=pl.CostEstimate(
            flops=12 * pairs * HEAD_DIM, bytes_accessed=4 * entered.size, transcendentals=pairs
        ),
        name="attention",
    )(counts, starts[:, None], entered, earlier)


def moves(copies, sems):
    started = [pltpu.make_async_copy(source, target, sems.at[i]) for i, (source, target) in enumerate(copies)]
    for copy in started:
        copy.start()
    for copy in started:
        copy.wait()


def portions(count, wholes, joined):
    pairs, at = [], 0
    for whole in wholes:
        width = whole.shape[1] // count
        for h in range(count):
            pairs.append((whole.at[:, pl.ds(h * width, width)], joined.at[h, :, pl.ds(at, width)]))
        at += width
    return pairs


def pack_kernel(count, *refs):
    *wholes, joined, sems = refs
    moves(portions(count, wholes, joined), sems)


def unpack_kernel(count, joined, *refs):
    *wholes, held, arrivals, sems = refs
    arriving = [pltpu.make_async_copy(joined.at[h], held.at[h], arrivals.at[h]) for h in range(count)]
    for copy in arriving:
        copy.start()
    leaving = portions(count, wholes, held)
    started = []
    for h in range(count):
        arriving[h].wait()
        for i in range(h, len(leaving), count):
            target, source = leaving[i]
            started.append(pltpu.make_async_copy(source, target, sems.at[i]))
            started[-1].start()
    for copy in started:
        copy.wait()


def pack(count, *wholes):
    rows = wholes[0].shape[0]
    width = sum(x.shape[1] for x in wholes) // count
    return pl.pallas_call(
        functools.partial(pack_kernel, count),
        in_specs=[pl.BlockSpec(memory_space=pl.ANY)] * len(wholes),
        out_specs=pl.BlockSpec(memory_space=pltpu.VMEM),
        out_shape=jax.ShapeDtypeStruct((count, rows, width), wholes[0].dtype),
        scratch_shapes=[pltpu.SemaphoreType.DMA((len(wholes) * count,))],
        name="pack",
    )(*wholes)


def unpack(joined, widths):
    count, rows, _ = joined.shape
    return pl.pallas_call(
        functools.partial(unpack_kernel, count),
        in_specs=[pl.BlockSpec(memory_space=pl.ANY)],
        out_specs=[pl.BlockSpec(memory_space=pl.ANY)] * len(widths),
        out_shape=[jax.ShapeDtypeStruct((rows, count * width), joined.dtype) for width in widths],
        scratch_shapes=[
            pltpu.VMEM(joined.shape, joined.dtype),
            pltpu.SemaphoreType.DMA((count,)),
            pltpu.SemaphoreType.DMA((len(widths) * count,)),
        ],
        name="unpack",
    )(joined)


def exchange(value):
    return lax.all_to_all(value, "head", split_axis=0, concat_axis=0, tiled=True)


def per_device(query, key, value, grad_out, doc_lengths):
    rows = query.shape[0]
    count = lax.axis_size("head")
    block = rows * count
    pair = 2 * HEAD_DIM
    middle = query.shape[1] // count

    packed = pack(count, query, grad_out, key, value)
    packed, place = lax.optimization_barrier((packed, lax.axis_index("blk")))
    entered, doc_lengths, place = lax.optimization_barrier((exchange(packed).reshape(block, -1), doc_lengths, place))
    doc_ends = jnp.cumsum(doc_lengths)
    doc_starts = doc_ends - doc_lengths
    origin = place * block - block
    positions = origin + block + jnp.arange(block, dtype=jnp.int32)
    starts = jnp.max(jnp.where(doc_starts[None, :] <= positions[:, None], doc_starts[None, :], 0), axis=1)
    starts = (starts - origin).astype(jnp.int32)
    earlier = passed_along(entered[:, 2 * middle :], "blk", 1)
    out, earlier_sums, own_sums = attention(entered, earlier, starts)
    returned = passed_along(earlier_sums, "blk", -1)
    pair_sums = (own_sums + returned.astype(jnp.float32)).astype(jnp.bfloat16)
    out = lax.dynamic_update_slice(out, pair_sums, (0, 2 * middle))
    back = exchange(out.reshape(count, rows, -1))
    return tuple(unpack(back, (middle, middle, HEAD_DIM, HEAD_DIM)))


def solution(mesh):
    spec = P(("blk", "head"), None)
    return jax.shard_map(
        per_device,
        mesh=mesh,
        in_specs=(spec, spec, spec, spec, P()),
        out_specs=(spec, spec, spec, spec),
        check_vma=False,
    )
```
